32 devices in a mesh: groups: 2 (over y), ctx: 8 (over z, core), heads: 2 (over x).
Axes of the slice: x: 2, y: 2, z: 4, core: 2. Of those that a mesh axis runs over, the one named last changes fastest.
Arguments:
- queries: bfloat16 [4096, 8192], P(('groups', 'ctx'), 'heads'), parts along dimension 0, may hold values from -32 to 32, as said below
- keys: bfloat16 [4096, 1024], P(('groups', 'ctx'), 'heads'), parts along dimension 0, may hold values from -32 to 32, as said below
- values: bfloat16 [4096, 1024], P(('groups', 'ctx'), 'heads'), parts along dimension 0, may hold values from -6 to 6
- doc_ids: int32 [4096], P('groups'), parts along dimension 0, may hold values from 0 to 17, never falling along the last dimension, each value on 1 to 1024 neighbouring positions
- block_mask: int32 [32, 16], P('groups'), parts along dimension 0, may hold values from 0 to 1, as said below
- out_weight: bfloat16 [8192, 8192], P('heads', 'ctx'), may hold values from -0.5 to 0.5
Outputs:
- mixed: bfloat16 [4096, 8192], P(('groups', 'ctx'), 'heads'), parts along dimension 0
The draws below stay inside these ranges and needn't reach their ends.
There are 2 independent parts, one for each index of `groups`. The reference program is written for one: setup_inputs(seed, part) draws one part's arguments, and reference() takes and returns one part's arrays. A program takes and returns all parts, laid end to end along the dimension named above; an argument that names none is the same for every part. Nothing has to cross between parts.
Inputs may be any that keep to these rules, and one draw needn't show every extreme that they name: `queries`: entries lie within the stated bounds. `keys`: entries lie within the stated bounds. `block_mask`: zero on and above the diagonal; the last block may read the first.
All inputs are finite; a program needn't handle non-finite values.
Results may differ from the reference program's by a relative error of at most 0.009.
Values may be sent and summed in bfloat16 or wider, within the bound.
No kernel may reach another device: no remote copies, remote signals or barrier semaphores. Data moves between devices by JAX's collectives and lax.ppermute only.
A program may use at most 256 MiB of HBM per device.

```python
import math
import jax
import jax.numpy as jnp
import numpy as np
from jax import lax

D = 8192
HEADS = 64
KVH = 8
HD = 128
BLOCK = 128
TOKENS = 2048
QW = 8192


def draw_queries(key, part):
    drawn = jnp.clip(jax.random.normal(jax.random.fold_in(key, 10), (TOKENS, HEADS * HD)), -6.0, 6.0)
    return drawn.astype(jnp.bfloat16)


def draw_keys(key, part):
    drawn = jnp.clip(jax.random.normal(jax.random.fold_in(key, 11), (TOKENS, KVH * HD)), -6.0, 6.0)
    return drawn.astype(jnp.bfloat16)


def draw_block_mask(key, part):
    count = TOKENS // BLOCK
    rolls = jax.random.randint(jax.random.fold_in(key, 20), (count, count), 0, 16)
    later = jnp.arange(count)[:, None]
    earlier = jnp.arange(count)[None, :]
    keep = jnp.where(earlier < max(count // 4, 1), rolls < 6, rolls < 1)
    keep = keep | (earlier == 0) & (later == count - 1)
    return jnp.where((earlier < later) & keep, 1, 0).astype(jnp.int32)


def shard_levels(own_key, extent, split, low, largest):
    gain = 1.0
    for axis_at, shards_of in split:
        steps = jax.random.uniform(jax.random.fold_in(jax.random.fold_in(own_key, 6), axis_at), (shards_of,), jnp.float32, low / len(split), largest / len(split))
        gain = gain * jnp.repeat(jnp.exp(steps), extent[axis_at] // shards_of).reshape((-1,) + (1,) * (len(extent) - 1 - axis_at))
    return gain


def length_profile(amount, total, bound, lean):
    loads = [(1 << 20) // math.isqrt(rank ** lean) + 1 for rank in range(2, amount + 1)]
    surplus, counts = total - bound - (amount - 1), [1] * (amount - 1)
    while surplus > 0:
        candidates = [i for i in range(amount - 1) if counts[i] < bound]
        whole, left = sum([loads[i] for i in candidates]), surplus
        for i in candidates:
            extra = min(bound - counts[i], max(1, left * loads[i] // whole), surplus)
            counts[i] = counts[i] + extra
            surplus = surplus - extra
    return np.array([bound] + counts)


def ragged_sizes(stream_key, amount, total, most, slope):
    if amount == 2:
        one = jax.random.randint(stream_key, (), max(1, total - most), min(most, total - 1) + 1)
        return jnp.stack([one, total - one])
    tallies = jnp.asarray(length_profile(amount, total, most, slope), jnp.int32)
    couples = (amount - 1) // 2
    donor, sink = tallies[1:1 + 2 * couples:2], tallies[2:2 + 2 * couples:2]
    margin = jnp.minimum(donor - 1, most - sink)
    shifted = jax.random.randint(jax.random.fold_in(stream_key, 1), (couples,), 0, 1 << 20) % (margin + 1)
    tallies = tallies.at[1:1 + 2 * couples:2].set(donor - shifted).at[2:2 + 2 * couples:2].set(sink + shifted)
    return tallies[jax.random.permutation(jax.random.fold_in(stream_key, 2), amount)]


def scatter_about(key, shape, scale, most, shards=(), held_as=jnp.bfloat16):
    entries = jax.random.normal(key, shape, jnp.float32) * scale
    if len(shards) > 0:
        entries = shard_levels(key, shape, shards, -0.22, 0.18) * entries
    return jnp.clip(entries, min=-most, max=most).astype(held_as)


def setup_inputs(seed: int = 0, part: int = 0) -> dict:
    key_of = jax.random.split(jax.random.key(seed), 7)
    own_keys = jax.random.split(jax.random.fold_in(key_of[6], part), 7)
    return {
        "queries": draw_queries(jax.random.fold_in(jax.random.fold_in(key_of[6], part), 71), part),
        "keys": draw_keys(jax.random.fold_in(jax.random.fold_in(key_of[6], part), 71), part),
        "values": scatter_about(own_keys[2], (TOKENS, KVH * HD), 1.0, 6.0, ((0, 8), (1, 2))),
        "doc_ids": jnp.searchsorted(jnp.cumsum(ragged_sizes(own_keys[3], TOKENS // 128 + 2, TOKENS, TOKENS // 2, 2)), jnp.arange(TOKENS), side="right").astype(jnp.int32),
        "block_mask": draw_block_mask(jax.random.fold_in(jax.random.fold_in(key_of[6], part), 71), part),
        "out_weight": scatter_about(key_of[5], (QW, D), (D // 64) ** -0.5, 0.5, ((0, 2), (1, 8))),
    }


def reference(queries, keys, values, doc_ids, block_mask, out_weight):
    group = HEADS // KVH
    scale = HD ** -0.5
    pos = jnp.arange(TOKENS, dtype=jnp.int32)
    blk = pos // BLOCK
    linked = block_mask[blk][:, blk] == 1
    allowed = (pos[None, :] <= pos[:, None]) & ((doc_ids[:, None] == doc_ids[None, :]) | linked)
    qall = queries.reshape(TOKENS, HEADS, HD).transpose(1, 0, 2)
    kall = keys.reshape(TOKENS, KVH, HD).transpose(1, 0, 2)
    vall = values.reshape(TOKENS, KVH, HD).transpose(1, 0, 2)

    def one_head(head):
        qhead = lax.dynamic_index_in_dim(qall, head, 0, keepdims=False)
        khead = lax.dynamic_index_in_dim(kall, head // group, 0, keepdims=False)
        vhead = lax.dynamic_index_in_dim(vall, head // group, 0, keepdims=False)
        scores = jnp.dot(qhead, khead.T, preferred_element_type=jnp.float32) * scale
        scores = jnp.where(allowed, scores, -1e30)
        peak = jnp.max(scores, axis=1, keepdims=True)
        expo = jnp.where(allowed, jnp.exp(scores - peak), 0.0)
        total = jnp.sum(expo, axis=1, keepdims=True)
        weighted = jnp.dot(expo.astype(jnp.bfloat16), vhead, preferred_element_type=jnp.float32)
        return (weighted / total).astype(jnp.bfloat16)

    outputs = lax.map(one_head, jnp.arange(HEADS, dtype=jnp.int32))
    attn = outputs.transpose(1, 0, 2).reshape(TOKENS, HEADS * HD)
    return jnp.dot(attn, out_weight, preferred_element_type=jnp.float32).astype(jnp.bfloat16)
```

```python
import functools
import jax, jax.numpy as jnp
from jax import lax
from jax.experimental import pallas as pl
from jax.experimental.pallas import tpu as pltpu
from jax.sharding import PartitionSpec as P

HEADS = 64
KVH = 8
GROUP = HEADS // KVH
HD = 128
BLOCK = 128
NEG = -1e30
LANES = ("ctx", "heads")

def attn_body(cores, meta, dlast, links, docq, dock, q, *rest):
    nkv = len(rest) - 6
    kvs = rest[:nkv]
    out, kv, acc, peak, todo, sem = rest[nkv:]
    heads_kv = pl.num_programs(0)
    j, b = pl.program_id(0), pl.program_id(1)
    per_dev = kv.shape[1]
    place = meta[0]
    core = lax.rem(place, cores)
    chip = lax.div(place, cores)
    nb = dlast.shape[0]
    hops = nkv // cores
    mine = place * per_dev + b

    @pl.when((j == 0) & (b == 0))
    def _():
        for i in range(nkv):
            for r in range(per_dev):
                pltpu.make_async_copy(kvs[i].at[pl.ds(r * BLOCK, BLOCK)], kv.at[i, r], sem.at[i, r]).start()
        for i in range(nkv):
            for r in range(per_dev):
                pltpu.make_async_copy(kvs[i].at[pl.ds(r * BLOCK, BLOCK)], kv.at[i, r], sem.at[i, r]).wait()

    todo[0] = mine
    def scan(t, n):
        on = (links[b * nb + t] > 0) | (dlast[t] == meta[1 + b])
        @pl.when(on)
        def _():
            todo[n] = t
        return n + on.astype(jnp.int32)
    count = lax.fori_loop(0, mine, scan, jnp.int32(1))
    todo[count] = mine

    acc[...] = jnp.zeros_like(acc)
    peak[...] = jnp.full_like(peak, NEG)
    dq = docq[...]
    rows = lax.broadcasted_iota(jnp.int32, (BLOCK, BLOCK), 0)
    cols = lax.broadcasted_iota(jnp.int32, (BLOCK, BLOCK), 1)
    c = HD ** -0.5 * 1.4426950408889634
    kcol = pl.ds(pl.multiple_of(j * HD, HD), HD)
    vcol = pl.ds(pl.multiple_of((heads_kv + j) * HD, HD), HD)

    def fetch(i):
        t = todo[i]
        dev = lax.div(t, per_dev)
        slot = (chip - lax.div(dev, cores)) + hops * (lax.rem(dev, cores) != core).astype(jnp.int32)
        r = lax.rem(t, per_dev)
        dk = dock[pl.ds(t, 1), :]
        ok = (dq == dk) | (links[b * nb + t] > 0)
        ok = ok & (rows + (mine - t) * BLOCK >= cols) & (i < count)
        return kv[slot, r, :, kcol], kv[slot, r, :, vcol], jnp.where(ok, 0.0, NEG)

    ones = jnp.ones((2 * BLOCK, HD), jnp.bfloat16)
    def step(i, carry):
        k0, v0, b0 = fetch(2 * i)
        k1, v1, b1 = fetch(2 * i + 1)
        keys = jnp.concatenate([k0, k1], 0)
        vals = jnp.concatenate([jnp.concatenate([v0, v1], 0), ones], 1)
        bias = jnp.concatenate([b0, b1], 1)
        for g in range(GROUP):
            s = lax.dot_general(q[:, g * HD:(g + 1) * HD], keys, (((1,), (1,)), ((), ())), preferred_element_type=jnp.float32)
            s = s + bias
            old = peak[g]
            top = jnp.maximum(old, jnp.max(s, axis=1, keepdims=True))
            fac = jnp.exp2((old - top) * c)
            p = jnp.exp2((s - jnp.concatenate([top, top], 1)) * c).astype(jnp.bfloat16)
            w = jnp.dot(p, vals, preferred_element_type=jnp.float32)
            acc[g] = acc[g] * jnp.concatenate([fac, fac], 1) + w
            peak[g] = top
        return carry
    lax.fori_loop(0, lax.div(count + 1, 2), step, 0)
    for g in range(GROUP):
        a = acc[g]
        out[:, g * HD:(g + 1) * HD] = (a[:, :HD] / a[:, HD:]).astype(out.dtype)

def attention(q, kvs, place, docs, mask, cores):
    tok, width = q.shape
    kvh = width // (GROUP * HD)
    per_dev = tok // BLOCK
    nb = mask.shape[0]
    dock = docs.reshape(nb, BLOCK)
    dlast = dock[:, -1]
    own = lax.dynamic_slice_in_dim(dock, place * per_dev, per_dev)
    meta = jnp.concatenate([place[None].astype(jnp.int32), own[:, 0]])
    links = lax.dynamic_slice_in_dim(mask, place * per_dev, per_dev).reshape(-1)
    docq = jnp.broadcast_to(own.reshape(tok, 1), (tok, BLOCK))
    n = len(kvs)
    grid_spec = pltpu.PrefetchScalarGridSpec(
        num_scalar_prefetch=3, grid=(kvh, per_dev),
        in_specs=[
            pl.BlockSpec((BLOCK, BLOCK), lambda j, b, *_: (b, 0)),
            pl.BlockSpec((nb, BLOCK), lambda j, b, *_: (0, 0)),
            pl.BlockSpec((BLOCK, GROUP * HD), lambda j, b, *_: (b, j)),
        ] + [pl.BlockSpec(memory_space=pl.ANY)] * n,
        out_specs=pl.BlockSpec((BLOCK, GROUP * HD), lambda j, b, *_: (b, j)),
        scratch_shapes=[
            pltpu.VMEM((n, per_dev, BLOCK, 2 * kvh * HD), jnp.bfloat16),
            pltpu.VMEM((GROUP, BLOCK, 2 * HD), jnp.float32),
            pltpu.VMEM((GROUP, BLOCK, HD), jnp.float32),
            pltpu.SMEM((nb + 2,), jnp.int32),
            pltpu.SemaphoreType.DMA((n, per_dev)),
        ])
    return pl.pallas_call(
        functools.partial(attn_body, cores), grid_spec=grid_spec,
        out_shape=jax.ShapeDtypeStruct((tok, width), jnp.bfloat16),
        name="attend",
        cost_estimate=pl.CostEstimate(flops=2*tok*width*nb*BLOCK, bytes_accessed=4 << 20, transcendentals=tok*width//HD*nb*BLOCK//2),
    )(meta, dlast, links, docq, dock, q, *kvs)


def project_body(meta, a0, b0, a1, b1, w0, w1, keep, send, left, sem):
    i = pl.program_id(0)
    half = left.shape[1] // 2

    @pl.when(i == 0)
    def _():
        def load(first, second):
            one = pltpu.make_async_copy(first, left.at[:, pl.ds(0, half)], sem.at[0])
            two = pltpu.make_async_copy(second, left.at[:, pl.ds(half, half)], sem.at[1])
            one.start()
            two.start()
            one.wait()
            two.wait()

        pl.when(meta[0] == 0)(lambda: load(a0, a1))
        pl.when(meta[0] != 0)(lambda: load(b0, b1))

    def store(w):
        res = jnp.dot(left[...], w[...], preferred_element_type=jnp.float32).astype(keep.dtype)
        rows = res.shape[0] // 2
        top, low = res[:rows], res[rows:]
        first = meta[1] == 0
        keep[...] = jnp.where(first, top, low)
        send[...] = jnp.where(first, low, top)

    tiles = pl.num_programs(0) // 2
    pl.when(i < tiles)(lambda: store(w0))
    pl.when(i >= tiles)(lambda: store(w1))


def project(pick, side, a, b, w0, w1, name):
    tok = a[0].shape[0]
    depth, cols = w0.shape
    step = 512
    tiles = cols // step
    meta = jnp.stack([pick.astype(jnp.int32), side.astype(jnp.int32)])
    spec = pl.BlockSpec(memory_space=pl.ANY)
    shape = jax.ShapeDtypeStruct((tok // 2, 2 * cols), jnp.bfloat16)
    grid_spec = pltpu.PrefetchScalarGridSpec(
        num_scalar_prefetch=1,
        grid=(2 * tiles,),
        in_specs=[spec] * 4
        + [
            pl.BlockSpec((depth, step), lambda i, *_: (0, jnp.minimum(i, tiles - 1))),
            pl.BlockSpec((depth, step), lambda i, *_: (0, jnp.maximum(i - tiles, 0))),
        ],
        out_specs=[pl.BlockSpec((tok // 2, step), lambda i, *_: (0, i))] * 2,
        scratch_shapes=[pltpu.VMEM((tok, depth), jnp.bfloat16), pltpu.SemaphoreType.DMA((2,))],
    )
    return pl.pallas_call(
        project_body,
        grid_spec=grid_spec,
        out_shape=[shape, shape],
        name=name,
        cost_estimate=pl.CostEstimate(
            flops=4 * tok * depth * cols, bytes_accessed=4 * depth * cols, transcendentals=0
        ),
        compiler_params=pltpu.CompilerParams(vmem_limit_bytes=40 << 20),
    )(meta, a[0], b[0], a[1], b[1], w0, w1)


def line(x, hop):
    n = lax.axis_size("ctx")
    pairs = [(i, i + 2 * hop) for i in range(n) if 0 <= i + 2 * hop < n]
    return lax.ppermute(x, "ctx", pairs)


def partner(x):
    return lax.ppermute(x, "ctx", [(i, i ^ 1) for i in range(lax.axis_size("ctx"))])


def across(x):
    return lax.ppermute(x, "heads", [(0, 1), (1, 0)])


def parts_of(keys, values, phases):
    width = keys.shape[1] // phases
    return [
        jnp.concatenate(
            [keys[:, f * width : (f + 1) * width], values[:, f * width : (f + 1) * width]], axis=1
        )
        for f in range(phases)
    ]


def on_line(queries, keys, values, doc_ids, block_mask, out_weight):
    place = lax.axis_index("ctx")
    side = lax.axis_index("heads")
    chip = place // 2
    core = place % 2
    home = chip // 2
    tok = queries.shape[0]
    phases = 2
    wide = queries.shape[1] // phases
    kv = parts_of(keys, values, phases)
    near = []
    for f in range(phases):
        one = line(kv[f], 1)
        two = line(kv[f], 2)
        three = line(two, 1)
        near.append([kv[f], one, two, three])
    w_other = partner(out_weight)
    attn, ups, downs = [], [[] for _ in range(3)], [[] for _ in range(3)]
    for f in range(phases):
        sources = near[f] + [partner(x) for x in near[f]]
        out = attention(
            queries[:, f * wide : (f + 1) * wide], sources, place, doc_ids, block_mask, 2
        )
        attn.append(out)
        up = down = out
        for s in range(3):
            up, down = line(up, 1), line(down, -1)
            ups[s].append(up)
            downs[s].append(down)

    low = chip < 2
    zero = jnp.int32(0)

    def slot(pick, a, b, name, hops):
        keep, send = project(pick, side, a, b, out_weight, w_other, name)
        total = keep + across(send)
        n = lax.axis_size("ctx")
        straight, crossed = [], []
        for z, t in hops:
            for k in range(2):
                for h in range(2):
                    to = (2 * t + k) * 2 + z // 2
                    pair = ((2 * z + k) * 2 + h, to)
                    (straight if h == z // 2 else crossed).append(pair)
        return lax.ppermute(total, LANES, straight), lax.ppermute(total, LANES, crossed)

    keep, send = project(zero, zero, attn, attn, out_weight, w_other, "project_own")
    goes = [((2 * z + k) * 2 + (1 - z // 2), (2 * z + k) * 2 + z // 2) for z in range(4) for k in range(2)]
    own = jnp.concatenate([keep, send], axis=0)
    own = own + lax.ppermute(own, LANES, goes)
    first = slot(~low, downs[0], ups[0], "project_1", [(0, 1), (1, 2), (2, 1), (3, 2)])
    again = slot(low, downs[0], ups[0], "project_1b", [(1, 0), (2, 3)])
    second = slot(~low, downs[1], ups[1], "project_2", [(0, 2), (1, 3), (2, 0), (3, 1)])
    third = slot(~low, downs[2], ups[2], "project_3", [(0, 3), (3, 0)])

    def rows(pair):
        straight, crossed = pair
        return jnp.where(
            side == 0,
            jnp.concatenate([straight, crossed], axis=0),
            jnp.concatenate([crossed, straight], axis=0),
        )

    came = {}
    for name, hops in (
        ("first", [(0, 1), (1, 2), (2, 1), (3, 2)]),
        ("again", [(1, 0), (2, 3)]),
        ("second", [(0, 2), (1, 3), (2, 0), (3, 1)]),
        ("third", [(0, 3), (3, 0)]),
        ("own", [(z, z) for z in range(4)]),
    ):
        for z, t in hops:
            came[(z, t)] = name
    got = {"first": rows(first), "again": rows(again), "second": rows(second), "third": rows(third), "own": own}
    pieces = []
    for i in range(2):
        piece = None
        for name, value in got.items():
            hit = jnp.bool_(False)
            for t in range(4):
                for h in range(2):
                    if came[(2 * h + i, t)] == name:
                        hit = hit | ((chip == t) & (side == h))
            piece = value if piece is None else jnp.where(hit, value, piece)
        cols = piece.shape[1] // 2
        swapped = jnp.concatenate([piece[:, cols:], piece[:, :cols]], axis=1)
        pieces.append(jnp.where(core == 0, piece, swapped))
    return jnp.concatenate(pieces, axis=1)


def gathered(queries, keys, values, doc_ids, block_mask, out_weight):
    place = lax.axis_index("ctx")
    n = lax.axis_size("ctx")
    kv = lax.all_gather(parts_of(keys, values, 1)[0], "ctx", axis=0)
    flip = place + 1 - 2 * (place % 2)

    def of(start):
        return [
            lax.dynamic_index_in_dim(kv, (start - 2 * s + n) % n, 0, keepdims=False)
            for s in range(n // 2)
        ]

    attn = attention(queries, of(place) + of(flip), place, doc_ids, block_mask, 2)
    partial_out = jnp.dot(
        attn,
        lax.all_gather(out_weight, "ctx", axis=1, tiled=True),
        preferred_element_type=jnp.float32,
    )
    return lax.psum_scatter(
        partial_out.astype(jnp.bfloat16), "heads", scatter_dimension=1, tiled=True
    )


def solution(mesh):
    in_specs = (
        P(("groups", "ctx"), "heads"),
        P(("groups", "ctx"), "heads"),
        P(("groups", "ctx"), "heads"),
        P("groups"),
        P("groups", None),
        P("heads", "ctx"),
    )
    out_specs = P(("groups", "ctx"), "heads")
    short = mesh.shape["ctx"] == 8 and mesh.shape["heads"] == 2
    return jax.shard_map(
        on_line if short else gathered,
        mesh=mesh,
        in_specs=in_specs,
        out_specs=out_specs,
        check_vma=False,
    )
```

```python
import functools
import jax, jax.numpy as jnp
from jax import lax
from jax.experimental import pallas as pl
from jax.experimental.pallas import tpu as pltpu
from jax.sharding import PartitionSpec as P


HEADS = 64
KVH = 8
GROUP = HEADS // KVH
TOGETHER = 4
HD = 128
BLOCK = 128
NEG = -1e30
LANES = ("ctx", "heads")


def attn_body(cores, skip, meta, dlast, links, docq, dock, q, *rest):
    nkv = len(rest) - 7
    kvs = rest[:nkv]
    out, kv, acc, peak, stack, todo, sem = rest[nkv:]
    j, b = pl.program_id(0), pl.program_id(1)
    per_dev = kv.shape[1]
    place = meta[0]
    core = lax.rem(place, cores)
    chip = lax.div(place, cores)
    nb = dlast.shape[0]
    hops = nkv // cores
    mine = place * per_dev + b

    @pl.when((j == 0) & (b == 0))
    def _():
        for i in range(nkv):
            for r in range(per_dev):
                pltpu.make_async_copy(kvs[i].at[pl.ds(r * BLOCK, BLOCK)], kv.at[i, r], sem.at[i, r]).start()
        for i in range(nkv):
            for r in range(per_dev):
                pltpu.make_async_copy(kvs[i].at[pl.ds(r * BLOCK, BLOCK)], kv.at[i, r], sem.at[i, r]).wait()

    @pl.when(j == 0)
    def _():
        todo[b, 0] = mine

        def scan(t, n):
            on = (links[b * nb + t] > 0) | (dlast[t] == meta[1 + b])
            todo[b, n] = t
            return n + on.astype(jnp.int32)

        n = lax.fori_loop(0, mine, scan, jnp.int32(1))
        todo[b, n] = mine
        todo[b, nb + 1] = n

    count = todo[b, nb + 1]

    acc[...] = jnp.zeros_like(acc)
    peak[...] = jnp.full_like(peak, NEG)
    for g in range(GROUP):
        stack[g * BLOCK : (g + 1) * BLOCK] = q[:, g * HD : (g + 1) * HD]
    dq = docq[...]
    rows = lax.broadcasted_iota(jnp.int32, (BLOCK, BLOCK), 0)
    cols = lax.broadcasted_iota(jnp.int32, (BLOCK, BLOCK), 1)
    c = HD ** -0.5 * 1.4426950408889634
    kcol = pl.ds(pl.multiple_of((skip + j) * HD, HD), HD)
    vcol = pl.ds(pl.multiple_of((kv.shape[3] // (2 * HD) + skip + j) * HD, HD), HD)

    def fetch(i):
        t = todo[b, i]
        dev = lax.div(t, per_dev)
        slot = (chip - lax.div(dev, cores)) + hops * (lax.rem(dev, cores) != core).astype(jnp.int32)
        r = lax.rem(t, per_dev)
        dk = dock[pl.ds(t, 1), :]
        ok = (dq == dk) | (links[b * nb + t] > 0)
        ok = ok & (rows + (mine - t) * BLOCK >= cols) & (i < count)
        return kv[slot, r, :, kcol], kv[slot, r, :, vcol], jnp.where(ok, 0.0, NEG)

    ones = jnp.ones((2 * BLOCK, HD), jnp.bfloat16)
    rows_of = TOGETHER * BLOCK

    def step(i, carry):
        k0, v0, b0 = fetch(2 * i)
        k1, v1, b1 = fetch(2 * i + 1)
        keys = jnp.concatenate([k0, k1], 0)
        vals = jnp.concatenate([jnp.concatenate([v0, v1], 0), ones], 1)
        bias = jnp.concatenate([b0, b1], 1)
        bias = jnp.concatenate([bias] * TOGETHER, 0)
        for g in range(GROUP // TOGETHER):
            at = slice(g * rows_of, (g + 1) * rows_of)
            s = lax.dot_general(stack[at], keys, (((1,), (1,)), ((), ())), preferred_element_type=jnp.float32)
            s = s + bias
            old = peak[at]
            top = jnp.maximum(old, jnp.max(s, axis=1, keepdims=True))
            fac = jnp.exp2((old - top) * c)
            p = jnp.exp2((s - jnp.concatenate([top, top], 1)) * c).astype(jnp.bfloat16)
            w = jnp.dot(p, vals, preferred_element_type=jnp.float32)
            acc[at] = acc[at] * jnp.concatenate([fac, fac], 1) + w
            peak[at] = top
        return carry

    lax.fori_loop(0, lax.div(count + 1, 2), step, 0)
    for g in range(GROUP):
        a = acc[g * BLOCK : (g + 1) * BLOCK]
        out[:, g * HD:(g + 1) * HD] = (a[:, :HD] / a[:, HD:]).astype(out.dtype)


def attention(q, kvs, place, docs, mask, cores, skip=0):
    tok, width = q.shape
    kvh = width // (GROUP * HD)
    per_dev = tok // BLOCK
    nb = mask.shape[0]
    dock = docs.reshape(nb, BLOCK)
    dlast = dock[:, -1]
    own = lax.dynamic_slice_in_dim(dock, place * per_dev, per_dev)
    meta = jnp.concatenate([place[None].astype(jnp.int32), own[:, 0]])
    links = lax.dynamic_slice_in_dim(mask, place * per_dev, per_dev).reshape(-1)
    docq = jnp.broadcast_to(own.reshape(tok, 1), (tok, BLOCK))
    n = len(kvs)
    grid_spec = pltpu.PrefetchScalarGridSpec(
        num_scalar_prefetch=3, grid=(kvh, per_dev),
        in_specs=[
            pl.BlockSpec((BLOCK, BLOCK), lambda j, b, *_: (b, 0)),
            pl.BlockSpec((nb, BLOCK), lambda j, b, *_: (0, 0)),
            pl.BlockSpec((BLOCK, GROUP * HD), lambda j, b, *_: (b, j)),
        ] + [pl.BlockSpec(memory_space=pl.ANY)] * n,
        out_specs=pl.BlockSpec((BLOCK, GROUP * HD), lambda j, b, *_: (b, j)),
        scratch_shapes=[
            pltpu.VMEM((n, per_dev, BLOCK, kvs[0].shape[1]), jnp.bfloat16),
            pltpu.VMEM((GROUP * BLOCK, 2 * HD), jnp.float32),
            pltpu.VMEM((GROUP * BLOCK, HD), jnp.float32),
            pltpu.VMEM((GROUP * BLOCK, HD), jnp.bfloat16),
            pltpu.SMEM((per_dev, nb + 2), jnp.int32),
            pltpu.SemaphoreType.DMA((n, per_dev)),
        ])
    return pl.pallas_call(
        functools.partial(attn_body, cores, skip), grid_spec=grid_spec,
        out_shape=jax.ShapeDtypeStruct((tok, width), jnp.bfloat16),
        name="attend",
        cost_estimate=pl.CostEstimate(flops=2*tok*width*nb*BLOCK, bytes_accessed=4 << 20, transcendentals=tok*width//HD*nb*BLOCK//2),
    )(meta, dlast, links, docq, dock, q, *kvs)


SENT = (2, 2)
UNITS = ((0, 0, 2), (1, 0, 2))


def project_body(mode, tiles, count, both, twin, meta, *rest):
    ins = rest[: 2 * count if both else count]
    rest = rest[len(ins) :]
    if mode == "rest":
        part, rest = rest[0], rest[1:]
    weights, rest = rest[: len(tiles)], rest[len(tiles) :]
    outs, (left, sem) = rest[:-2], rest[-2:]
    i = pl.program_id(0)
    half = left.shape[1] // count

    @pl.when(i == 0)
    def _():
        def load(group):
            tok = group[0].shape[0]
            copies = [
                pltpu.make_async_copy(
                    x,
                    left.at[pl.ds(n // count * tok, tok), pl.ds(n % count * half, half)],
                    sem.at[n],
                )
                for n, x in enumerate(group)
            ]
            for copy in copies:
                copy.start()
            for copy in copies:
                copy.wait()

        if not both:
            load(ins)
        else:
            one, two = ins[:count], ins[count:]
            pl.when(meta[0] == 0)(lambda: load(one + two if twin else one))
            pl.when(meta[0] != 0)(lambda: load(two + one if twin else two))

    def store(w):
        res = jnp.dot(left[...], w[...], preferred_element_type=jnp.float32)
        if mode == "rest":
            res = res + part[...]
        if mode in ("full", "part"):
            outs[0][...] = res.astype(outs[0].dtype)
            return
        res = res.astype(jnp.bfloat16)
        rows = res.shape[0] // (4 if twin else 2)
        first = meta[1] == 0
        for n in range(2 if twin else 1):
            at = slice(n * rows, (n + 1) * rows)
            top, low = res[2 * n * rows : (2 * n + 1) * rows], res[(2 * n + 1) * rows : (2 * n + 2) * rows]
            outs[0][at] = jnp.where(first, top, low)
            outs[1][at] = jnp.where(first, low, top)

    begin = 0
    for w, n in zip(weights, tiles):
        pl.when((i >= begin) & (i < begin + n))(lambda w=w: store(w))
        begin += n


def project(mode, pick, side, a, b, weights, row=None, part=None, twin=False):
    tok = a[0].shape[0] * (2 if twin else 1)
    cols = weights[0].shape[1]
    depth = sum(x.shape[1] for x in a)
    at = 0 if row is None else row
    step = 512
    per = cols // step
    tiles = [per] * len(weights)
    total = cols * len(weights)
    meta = jnp.stack([pick.astype(jnp.int32), side.astype(jnp.int32)])
    anywhere = pl.BlockSpec(memory_space=pl.ANY)
    ins = list(a) + list(b)
    specs = [anywhere] * len(ins)
    if part is not None:
        array, first = part
        ins.append(array)
        specs.append(pl.BlockSpec((tok, step), lambda i, *_: (0, first + i)))
    for n, w in enumerate(weights):
        ins.append(w)
        specs.append(
            pl.BlockSpec((depth, step), lambda i, *_, n=n: (at, jnp.clip(i - n * per, 0, per - 1)))
        )
    if mode in ("full", "part"):
        kind = jnp.bfloat16 if mode == "full" else jnp.float32
        outs = jax.ShapeDtypeStruct((tok, total), kind)
        out_specs = pl.BlockSpec((tok, step), lambda i, *_: (0, i))
    else:
        outs = [jax.ShapeDtypeStruct((tok // 2, total), jnp.bfloat16)] * 2
        out_specs = [pl.BlockSpec((tok // 2, step), lambda i, *_: (0, i))] * 2
    grid_spec = pltpu.PrefetchScalarGridSpec(
        num_scalar_prefetch=1,
        grid=(per * len(weights),),
        in_specs=specs,
        out_specs=out_specs,
        scratch_shapes=[
            pltpu.VMEM((tok, depth), jnp.bfloat16),
            pltpu.SemaphoreType.DMA((2 * len(a),)),
        ],
    )
    return pl.pallas_call(
        functools.partial(project_body, mode, tiles, len(a), bool(b), twin),
        grid_spec=grid_spec,
        out_shape=outs,
        cost_estimate=pl.CostEstimate(
            flops=2 * tok * depth * total, bytes_accessed=2 * depth * total, transcendentals=0
        ),
        compiler_params=pltpu.CompilerParams(vmem_limit_bytes=40 << 20),
    )(meta, *ins)


NAMES = ("first", "again", "second", "third", "own")
HOPS = {
    "first": [(0, 1), (1, 2), (2, 1), (3, 2)],
    "again": [(1, 0), (2, 3)],
    "second": [(0, 2), (1, 3), (2, 0), (3, 1)],
    "third": [(0, 3), (3, 0)],
    "own": [(z, z) for z in range(4)],
}


def spots_of(name, piece):
    return [(h, t) for h in range(2) for t in range(4) if (2 * h + piece, t) in HOPS[name]]


def any_of(spots, chip, side):
    return functools.reduce(jnp.logical_or, [(chip == t) & (side == h) for h, t in spots])


def block_at(out, core, side, piece, other, row):
    rows, cols = out.shape[0] // 2, out.shape[1] // 4
    block = piece * 2 + jnp.where(core == 0, other, 1 - other)
    at = pl.ds(pl.multiple_of(block * cols, cols), cols)
    if row is None:
        return out.at[:, at]
    half = side if row == 0 else 1 - side
    return out.at[pl.ds(pl.multiple_of(half * rows, rows), rows), at]


def collect_body(meta, *refs):
    ins, (out, sem) = refs[:-2], refs[-2:]
    got = {n: ins[2 * i : 2 * i + 2] for i, n in enumerate(NAMES[:3])}
    own = ins[6]
    chip, side, core = meta[0], meta[1], meta[2]
    cols = out.shape[1] // 4

    def copies(name, piece):
        made = []
        for o in range(2):
            at = pl.ds(o * cols, cols)
            if name == "own":
                dst = block_at(out, core, side, piece, o, None)
                made.append(pltpu.make_async_copy(own.at[:, at], dst, sem.at[piece, o]))
                continue
            for r in range(2):
                dst = block_at(out, core, side, piece, o, r)
                src = got[name][r].at[:, at]
                made.append(pltpu.make_async_copy(src, dst, sem.at[piece, 2 * o + r]))
        return made

    todo = [(p, n) for p in range(2) for n in ("first", "again", "second", "own")]
    todo = [(p, n, any_of(spots_of(n, p), chip, side)) for p, n in todo if spots_of(n, p)]
    for p, n, hit in todo:
        pl.when(hit)(lambda p=p, n=n: [c.start() for c in copies(n, p)] and None)
    for p, n, hit in todo:
        pl.when(hit)(lambda p=p, n=n: [c.wait() for c in copies(n, p)] and None)


def finish_body(meta, *refs):
    third, (_, out, held, sem) = refs[:4], refs[4:]
    chip, side, core = meta[0], meta[1], meta[2]
    for piece in range(2):
        spots = spots_of("third", piece)

        @pl.when(any_of(spots, chip, side))
        def _(piece=piece):
            into = [
                pltpu.make_async_copy(third[n], held.at[n], sem.at[n]) for n in range(4)
            ]
            back = [
                pltpu.make_async_copy(
                    held.at[n], block_at(out, core, side, piece, n // 2, n % 2), sem.at[n]
                )
                for n in range(4)
            ]
            for copy in into:
                copy.start()
            for one, two in zip(into, back):
                one.wait()
                two.start()
            for copy in back:
                copy.wait()


def collect(chip, side, core, arrays, tok, cols):
    meta = jnp.stack([chip, side, core]).astype(jnp.int32)
    return pl.pallas_call(
        collect_body,
        grid_spec=pltpu.PrefetchScalarGridSpec(
            num_scalar_prefetch=1,
            grid=(),
            in_specs=[pl.BlockSpec(memory_space=pl.ANY)] * len(arrays),
            out_specs=pl.BlockSpec((tok, cols), lambda *_: (0, 0)),
            scratch_shapes=[pltpu.SemaphoreType.DMA((2, 4))],
        ),
        out_shape=jax.ShapeDtypeStruct((tok, cols), jnp.bfloat16),
        name="collect",
    )(meta, *arrays)


def finish(chip, side, core, arrays, out):
    meta = jnp.stack([chip, side, core]).astype(jnp.int32)
    anywhere = pl.BlockSpec(memory_space=pl.ANY)
    return pl.pallas_call(
        finish_body,
        grid_spec=pltpu.PrefetchScalarGridSpec(
            num_scalar_prefetch=1,
            grid=(),
            in_specs=[anywhere] * (len(arrays) + 1),
            out_specs=anywhere,
            scratch_shapes=[
                pltpu.VMEM((4,) + arrays[0].shape, jnp.bfloat16),
                pltpu.SemaphoreType.DMA((4,)),
            ],
        ),
        out_shape=jax.ShapeDtypeStruct(out.shape, out.dtype),
        input_output_aliases={len(arrays) + 1: 0},
        name="finish",
    )(meta, *arrays, out)


def line(x, hop):
    n = lax.axis_size("ctx")
    pairs = [(i, i + 2 * hop) for i in range(n) if 0 <= i + 2 * hop < n]
    return lax.ppermute(x, "ctx", pairs)


def partner(x):
    return lax.ppermute(x, "ctx", [(i, i ^ 1) for i in range(lax.axis_size("ctx"))])


def across(x):
    return lax.ppermute(x, "heads", [(0, 1), (1, 0)])


def parts_of(keys, values, heads):
    out, at = [], 0
    for n in heads:
        cut = slice(at * HD, (at + n) * HD)
        out.append(jnp.concatenate([keys[:, cut], values[:, cut]], axis=1))
        at += n
    return out


def send_back(slot, total):
    straight, crossed = [], []
    for z, t in HOPS[slot]:
        for k in range(2):
            for h in range(2):
                pair = ((2 * z + k) * 2 + h, (2 * t + k) * 2 + z // 2)
                (straight if h == z // 2 else crossed).append(pair)
    one = lax.ppermute(total, LANES, straight)
    two = lax.ppermute(total, LANES, crossed)
    return one, two


def on_line(queries, keys, values, doc_ids, block_mask, out_weight):
    place = lax.axis_index("ctx")
    side = lax.axis_index("heads")
    chip = place // 2
    core = place % 2
    tok = queries.shape[0]
    kv = parts_of(keys, values, SENT)
    near = [[kv[f]] + [line(kv[f], s) for s in range(1, 4)] for f in range(len(kv))]
    w_other = partner(out_weight)
    whole = [near[f] + [partner(x) for x in near[f]] for f in range(len(kv))]
    attn, ups, downs = [], [[] for _ in range(3)], [[] for _ in range(3)]
    left = 0
    for f, skip, n in UNITS:
        wide = n * GROUP * HD
        out = attention(
            queries[:, left : left + wide], whole[f], place, doc_ids, block_mask, 2, skip
        )
        left += wide
        attn.append(out)
        up = down = out
        for s in range(3):
            up = line(up, 1)
            down = line(down, -1)
            ups[s].append(up)
            downs[s].append(down)

    low = chip < 2
    zero = jnp.int32(0)
    pair = [out_weight, w_other]

    own = project("full", zero, zero, attn, [], pair)
    goes = [
        ((2 * z + k) * 2 + (1 - z // 2), (2 * z + k) * 2 + z // 2)
        for z in range(4)
        for k in range(2)
    ]
    moved = lax.ppermute(own, LANES, goes)
    arrays = []
    keep, send = project("split", ~low, side, downs[0], ups[0], pair, twin=True)
    both = keep + across(send)
    arrays += send_back("first", both[: tok // 2])
    arrays += send_back("again", both[tok // 2 :])
    keep, send = project("split", ~low, side, downs[1], ups[1], pair)
    arrays += send_back("second", keep + across(send))
    own = own + moved
    out = collect(chip, side, core, arrays + [own], tok, queries.shape[1])
    early = project("part", ~low, side, downs[2][:-1], ups[2][:-1], pair, row=0)
    cols = out_weight.shape[1]
    thirds = []
    for o in range(2):
        keep, send = project(
            "rest",
            ~low,
            side,
            downs[2][-1:],
            ups[2][-1:],
            pair[o : o + 1],
            row=1,
            part=(early, o * cols // 512),
        )
        thirds += send_back("third", keep + across(send))
    return finish(chip, side, core, thirds, out)


def gathered(queries, keys, values, doc_ids, block_mask, out_weight):
    place = lax.axis_index("ctx")
    n = lax.axis_size("ctx")
    kv = lax.all_gather(parts_of(keys, values, [keys.shape[1] // HD])[0], "ctx", axis=0)
    flip = place + 1 - 2 * (place % 2)

    def of(start):
        return [
            lax.dynamic_index_in_dim(kv, (start - 2 * s + n) % n, 0, keepdims=False)
            for s in range(n // 2)
        ]

    attn = attention(queries, of(place) + of(flip), place, doc_ids, block_mask, 2)
    partial_out = jnp.dot(
        attn,
        lax.all_gather(out_weight, "ctx", axis=1, tiled=True),
        preferred_element_type=jnp.float32,
    )
    return lax.psum_scatter(
        partial_out.astype(jnp.bfloat16), "heads", scatter_dimension=1, tiled=True
    )


def solution(mesh):
    in_specs = (
        P(("groups", "ctx"), "heads"),
        P(("groups", "ctx"), "heads"),
        P(("groups", "ctx"), "heads"),
        P("groups"),
        P("groups", None),
        P("heads", "ctx"),
    )
    out_specs = P(("groups", "ctx"), "heads")
    short = mesh.shape["ctx"] == 8 and mesh.shape["heads"] == 2

    def body(*args):
        return (on_line if short else gathered)(*args)

    return jax.shard_map(
        body, mesh=mesh, in_specs=in_specs, out_specs=out_specs, check_vma=False
    )
```

```python
import functools
import jax, jax.numpy as jnp
from jax import lax
from jax.experimental import pallas as pl
from jax.experimental.pallas import tpu as pltpu
from jax.sharding import PartitionSpec as P


HEADS = 64
KVH = 8
GROUP = HEADS // KVH
TOGETHER = 4
HD = 128
BLOCK = 128
NEG = -1e30
LANES = ("ctx", "heads")


def attn_body(cores, skip, meta, dlast, links, docq, dock, q, *rest):
    nkv = len(rest) - 7
    kvs = rest[:nkv]
    out, kv, acc, peak, stack, todo, sem = rest[nkv:]
    j, b = pl.program_id(0), pl.program_id(1)
    per_dev = kv.shape[1]
    place = meta[0]
    core = lax.rem(place, cores)
    chip = lax.div(place, cores)
    nb = dlast.shape[0]
    hops = nkv // cores
    mine = place * per_dev + b

    @pl.when((j == 0) & (b == 0))
    def _():
        for i in range(nkv):
            for r in range(per_dev):
                pltpu.make_async_copy(kvs[i].at[pl.ds(r * BLOCK, BLOCK)], kv.at[i, r], sem.at[i, r]).start()
        for i in range(nkv):
            for r in range(per_dev):
                pltpu.make_async_copy(kvs[i].at[pl.ds(r * BLOCK, BLOCK)], kv.at[i, r], sem.at[i, r]).wait()

    @pl.when(j == 0)
    def _():
        todo[b, 0] = mine

        def scan(t, n):
            on = (links[b * nb + t] > 0) | (dlast[t] == meta[1 + b])
            todo[b, n] = t
            return n + on.astype(jnp.int32)

        n = lax.fori_loop(0, mine, scan, jnp.int32(1))
        todo[b, n] = mine
        todo[b, nb + 1] = n

    count = todo[b, nb + 1]

    acc[...] = jnp.zeros_like(acc)
    peak[...] = jnp.full_like(peak, NEG)
    for g in range(GROUP):
        stack[g * BLOCK : (g + 1) * BLOCK] = q[:, g * HD : (g + 1) * HD]
    dq = docq[...]
    rows = lax.broadcasted_iota(jnp.int32, (BLOCK, BLOCK), 0)
    cols = lax.broadcasted_iota(jnp.int32, (BLOCK, BLOCK), 1)
    c = HD ** -0.5 * 1.4426950408889634
    kcol = pl.ds(pl.multiple_of((skip + j) * HD, HD), HD)
    vcol = pl.ds(pl.multiple_of((kv.shape[3] // (2 * HD) + skip + j) * HD, HD), HD)

    def fetch(i):
        t = todo[b, i]
        dev = lax.div(t, per_dev)
        slot = (chip - lax.div(dev, cores)) + hops * (lax.rem(dev, cores) != core).astype(jnp.int32)
        r = lax.rem(t, per_dev)
        dk = dock[pl.ds(t, 1), :]
        ok = (dq == dk) | (links[b * nb + t] > 0)
        ok = ok & (rows + (mine - t) * BLOCK >= cols) & (i < count)
        return kv[slot, r, :, kcol], kv[slot, r, :, vcol], jnp.where(ok, 0.0, NEG)

    ones = jnp.ones((2 * BLOCK, HD), jnp.bfloat16)
    rows_of = TOGETHER * BLOCK

    def step(i, carry):
        k0, v0, b0 = fetch(2 * i)
        k1, v1, b1 = fetch(2 * i + 1)
        keys = jnp.concatenate([k0, k1], 0)
        vals = jnp.concatenate([jnp.concatenate([v0, v1], 0), ones], 1)
        bias = jnp.concatenate([b0, b1], 1)
        bias = jnp.concatenate([bias] * TOGETHER, 0)
        for g in range(GROUP // TOGETHER):
            at = slice(g * rows_of, (g + 1) * rows_of)
            s = lax.dot_general(stack[at], keys, (((1,), (1,)), ((), ())), preferred_element_type=jnp.float32)
            s = s + bias
            old = peak[at]
            top = jnp.maximum(old, jnp.max(s, axis=1, keepdims=True))
            fac = jnp.exp2((old - top) * c)
            p = jnp.exp2((s - jnp.concatenate([top, top], 1)) * c).astype(jnp.bfloat16)
            w = jnp.dot(p, vals, preferred_element_type=jnp.float32)
            acc[at] = acc[at] * jnp.concatenate([fac, fac], 1) + w
            peak[at] = top
        return carry

    lax.fori_loop(0, lax.div(count + 1, 2), step, 0)
    for g in range(GROUP):
        a = acc[g * BLOCK : (g + 1) * BLOCK]
        out[:, g * HD:(g + 1) * HD] = (a[:, :HD] / a[:, HD:]).astype(out.dtype)


def attention(q, kvs, place, docs, mask, cores, skip=0):
    tok, width = q.shape
    kvh = width // (GROUP * HD)
    per_dev = tok // BLOCK
    nb = mask.shape[0]
    dock = docs.reshape(nb, BLOCK)
    dlast = dock[:, -1]
    own = lax.dynamic_slice_in_dim(dock, place * per_dev, per_dev)
    meta = jnp.concatenate([place[None].astype(jnp.int32), own[:, 0]])
    links = lax.dynamic_slice_in_dim(mask, place * per_dev, per_dev).reshape(-1)
    docq = jnp.broadcast_to(own.reshape(tok, 1), (tok, BLOCK))
    n = len(kvs)
    grid_spec = pltpu.PrefetchScalarGridSpec(
        num_scalar_prefetch=3, grid=(kvh, per_dev),
        in_specs=[
            pl.BlockSpec((BLOCK, BLOCK), lambda j, b, *_: (b, 0)),
            pl.BlockSpec((nb, BLOCK), lambda j, b, *_: (0, 0)),
            pl.BlockSpec((BLOCK, GROUP * HD), lambda j, b, *_: (b, j)),
        ] + [pl.BlockSpec(memory_space=pl.ANY)] * n,
        out_specs=pl.BlockSpec((BLOCK, GROUP * HD), lambda j, b, *_: (b, j)),
        scratch_shapes=[
            pltpu.VMEM((n, per_dev, BLOCK, kvs[0].shape[1]), jnp.bfloat16),
            pltpu.VMEM((GROUP * BLOCK, 2 * HD), jnp.float32),
            pltpu.VMEM((GROUP * BLOCK, HD), jnp.float32),
            pltpu.VMEM((GROUP * BLOCK, HD), jnp.bfloat16),
            pltpu.SMEM((per_dev, nb + 2), jnp.int32),
            pltpu.SemaphoreType.DMA((n, per_dev)),
        ])
    return pl.pallas_call(
        functools.partial(attn_body, cores, skip), grid_spec=grid_spec,
        out_shape=jax.ShapeDtypeStruct((tok, width), jnp.bfloat16),
        name="attend",
        cost_estimate=pl.CostEstimate(flops=2*tok*width*nb*BLOCK, bytes_accessed=4 << 20, transcendentals=tok*width//HD*nb*BLOCK//2),
    )(meta, dlast, links, docq, dock, q, *kvs)


SENT = (2, 2)
UNITS = ((0, 0, 2), (1, 0, 2))


def project_body(mode, tiles, count, both, twin, meta, *rest):
    ins = rest[: 2 * count if both else count]
    rest = rest[len(ins) :]
    if mode == "rest":
        part, rest = rest[0], rest[1:]
    weights, rest = rest[: len(tiles)], rest[len(tiles) :]
    outs, (left, sem) = rest[:-2], rest[-2:]
    i = pl.program_id(0)
    half = left.shape[1] // count

    @pl.when(i == 0)
    def _():
        def load(group):
            tok = group[0].shape[0]
            copies = [
                pltpu.make_async_copy(
                    x,
                    left.at[pl.ds(n // count * tok, tok), pl.ds(n % count * half, half)],
                    sem.at[n],
                )
                for n, x in enumerate(group)
            ]
            for copy in copies:
                copy.start()
            for copy in copies:
                copy.wait()

        if not both:
            load(ins)
        else:
            one, two = ins[:count], ins[count:]
            pl.when(meta[0] == 0)(lambda: load(one + two if twin else one))
            pl.when(meta[0] != 0)(lambda: load(two + one if twin else two))

    def store(w):
        res = jnp.dot(left[...], w[...], preferred_element_type=jnp.float32)
        if mode == "rest":
            res = res + part[...]
        if mode in ("full", "part"):
            outs[0][...] = res.astype(outs[0].dtype)
            return
        res = res.astype(jnp.bfloat16)
        rows = res.shape[0] // (4 if twin else 2)
        first = meta[1] == 0
        for n in range(2 if twin else 1):
            at = slice(n * rows, (n + 1) * rows)
            top, low = res[2 * n * rows : (2 * n + 1) * rows], res[(2 * n + 1) * rows : (2 * n + 2) * rows]
            outs[0][at] = jnp.where(first, top, low)
            outs[1][at] = jnp.where(first, low, top)

    begin = 0
    for w, n in zip(weights, tiles):
        pl.when((i >= begin) & (i < begin + n))(lambda w=w: store(w))
        begin += n


def project(mode, pick, side, a, b, weights, row=None, part=None, twin=False):
    tok = a[0].shape[0] * (2 if twin else 1)
    cols = weights[0].shape[1]
    depth = sum(x.shape[1] for x in a)
    at = 0 if row is None else row
    step = 512
    per = cols // step
    tiles = [per] * len(weights)
    total = cols * len(weights)
    meta = jnp.stack([pick.astype(jnp.int32), side.astype(jnp.int32)])
    anywhere = pl.BlockSpec(memory_space=pl.ANY)
    ins = list(a) + list(b)
    specs = [anywhere] * len(ins)
    if part is not None:
        array, first = part
        ins.append(array)
        specs.append(pl.BlockSpec((tok, step), lambda i, *_: (0, first + i)))
    for n, w in enumerate(weights):
        ins.append(w)
        specs.append(
            pl.BlockSpec((depth, step), lambda i, *_, n=n: (at, jnp.clip(i - n * per, 0, per - 1)))
        )
    if mode in ("full", "part"):
        kind = jnp.bfloat16 if mode == "full" else jnp.float32
        outs = jax.ShapeDtypeStruct((tok, total), kind)
        out_specs = pl.BlockSpec((tok, step), lambda i, *_: (0, i))
    else:
        outs = [jax.ShapeDtypeStruct((tok // 2, total), jnp.bfloat16)] * 2
        out_specs = [pl.BlockSpec((tok // 2, step), lambda i, *_: (0, i))] * 2
    grid_spec = pltpu.PrefetchScalarGridSpec(
        num_scalar_prefetch=1,
        grid=(per * len(weights),),
        in_specs=specs,
        out_specs=out_specs,
        scratch_shapes=[
            pltpu.VMEM((tok, depth), jnp.bfloat16),
            pltpu.SemaphoreType.DMA((2 * len(a),)),
        ],
    )
    return pl.pallas_call(
        functools.partial(project_body, mode, tiles, len(a), bool(b), twin),
        grid_spec=grid_spec,
        out_shape=outs,
        cost_estimate=pl.CostEstimate(
            flops=2 * tok * depth * total, bytes_accessed=2 * depth * total, transcendentals=0
        ),
        compiler_params=pltpu.CompilerParams(vmem_limit_bytes=40 << 20),
    )(meta, *ins)


NAMES = ("first", "again", "second", "third", "own")
HOPS = {
    "first": [(0, 1), (1, 2), (2, 1), (3, 2)],
    "again": [(1, 0), (2, 3)],
    "second": [(0, 2), (1, 3), (2, 0), (3, 1)],
    "third": [(0, 3), (3, 0)],
    "own": [(z, z) for z in range(4)],
}


def spots_of(name, piece):
    return [(h, t) for h in range(2) for t in range(4) if (2 * h + piece, t) in HOPS[name]]


def any_of(spots, chip, side):
    return functools.reduce(jnp.logical_or, [(chip == t) & (side == h) for h, t in spots])


def block_at(out, core, side, piece, other, row):
    rows, cols = out.shape[0] // 2, out.shape[1] // 4
    block = piece * 2 + jnp.where(core == 0, other, 1 - other)
    at = pl.ds(pl.multiple_of(block * cols, cols), cols)
    if row is None:
        return out.at[:, at]
    half = side if row == 0 else 1 - side
    return out.at[pl.ds(pl.multiple_of(half * rows, rows), rows), at]


def collect_body(meta, *refs):
    ins, (out, sem) = refs[:-2], refs[-2:]
    got = {n: ins[2 * i : 2 * i + 2] for i, n in enumerate(NAMES[:3])}
    own = ins[6]
    chip, side, core = meta[0], meta[1], meta[2]
    cols = out.shape[1] // 4

    def copies(name, piece):
        made = []
        for o in range(2):
            at = pl.ds(o * cols, cols)
            if name == "own":
                dst = block_at(out, core, side, piece, o, None)
                made.append(pltpu.make_async_copy(own.at[:, at], dst, sem.at[piece, o]))
                continue
            for r in range(2):
                dst = block_at(out, core, side, piece, o, r)
                src = got[name][r].at[:, at]
                made.append(pltpu.make_async_copy(src, dst, sem.at[piece, 2 * o + r]))
        return made

    todo = [(p, n) for p in range(2) for n in ("first", "again", "second", "own")]
    todo = [(p, n, any_of(spots_of(n, p), chip, side)) for p, n in todo if spots_of(n, p)]
    for p, n, hit in todo:
        pl.when(hit)(lambda p=p, n=n: [c.start() for c in copies(n, p)] and None)
    for p, n, hit in todo:
        pl.when(hit)(lambda p=p, n=n: [c.wait() for c in copies(n, p)] and None)


def finish_body(meta, *refs):
    third, (_, out, held, sem) = refs[:2], refs[2:]
    chip, side, core = meta[0], meta[1], meta[2]
    cols = out.shape[1] // 4
    for piece in range(2):
        spots = spots_of("third", piece)

        @pl.when(any_of(spots, chip, side))
        def _(piece=piece):
            into, back = [], []
            for n in range(4):
                o, r = n // 2, n % 2
                src = third[r].at[:, pl.ds(o * cols, cols)]
                into.append(pltpu.make_async_copy(src, held.at[n], sem.at[n]))
                dst = block_at(out, core, side, piece, o, r)
                back.append(pltpu.make_async_copy(held.at[n], dst, sem.at[n]))
            for copy in into:
                copy.start()
            for one, two in zip(into, back):
                one.wait()
                two.start()
            for copy in back:
                copy.wait()


def collect(chip, side, core, arrays, tok, cols):
    meta = jnp.stack([chip, side, core]).astype(jnp.int32)
    return pl.pallas_call(
        collect_body,
        grid_spec=pltpu.PrefetchScalarGridSpec(
            num_scalar_prefetch=1,
            grid=(),
            in_specs=[pl.BlockSpec(memory_space=pl.ANY)] * len(arrays),
            out_specs=pl.BlockSpec((tok, cols), lambda *_: (0, 0)),
            scratch_shapes=[pltpu.SemaphoreType.DMA((2, 4))],
        ),
        out_shape=jax.ShapeDtypeStruct((tok, cols), jnp.bfloat16),
        name="collect",
    )(meta, *arrays)


def finish(chip, side, core, arrays, out):
    meta = jnp.stack([chip, side, core]).astype(jnp.int32)
    anywhere = pl.BlockSpec(memory_space=pl.ANY)
    return pl.pallas_call(
        finish_body,
        grid_spec=pltpu.PrefetchScalarGridSpec(
            num_scalar_prefetch=1,
            grid=(),
            in_specs=[anywhere] * (len(arrays) + 1),
            out_specs=anywhere,
            scratch_shapes=[
                pltpu.VMEM((4, out.shape[0] // 2, out.shape[1] // 4), jnp.bfloat16),
                pltpu.SemaphoreType.DMA((4,)),
            ],
        ),
        out_shape=jax.ShapeDtypeStruct(out.shape, out.dtype),
        input_output_aliases={len(arrays) + 1: 0},
        name="finish",
    )(meta, *arrays, out)


def line(x, hop):
    n = lax.axis_size("ctx")
    pairs = [(i, i + 2 * hop) for i in range(n) if 0 <= i + 2 * hop < n]
    return lax.ppermute(x, "ctx", pairs)


def partner(x):
    return lax.ppermute(x, "ctx", [(i, i ^ 1) for i in range(lax.axis_size("ctx"))])


def across(x):
    return lax.ppermute(x, "heads", [(0, 1), (1, 0)])


def parts_of(keys, values, heads):
    out, at = [], 0
    for n in heads:
        cut = slice(at * HD, (at + n) * HD)
        out.append(jnp.concatenate([keys[:, cut], values[:, cut]], axis=1))
        at += n
    return out


def send_back(slot, total):
    straight, crossed = [], []
    for z, t in HOPS[slot]:
        for k in range(2):
            for h in range(2):
                pair = ((2 * z + k) * 2 + h, (2 * t + k) * 2 + z // 2)
                (straight if h == z // 2 else crossed).append(pair)
    one = lax.ppermute(total, LANES, straight)
    two = lax.ppermute(total, LANES, crossed)
    return one, two


def on_line(queries, keys, values, doc_ids, block_mask, out_weight):
    place = lax.axis_index("ctx")
    side = lax.axis_index("heads")
    chip = place // 2
    core = place % 2
    tok = queries.shape[0]
    kv = parts_of(keys, values, SENT)
    near = [[kv[f]] + [line(kv[f], s) for s in range(1, 4)] for f in range(len(kv))]
    w_other = partner(out_weight)
    whole = [near[f] + [partner(x) for x in near[f]] for f in range(len(kv))]
    attn, ups, downs = [], [[] for _ in range(3)], [[] for _ in range(3)]
    left = 0
    for f, skip, n in UNITS:
        wide = n * GROUP * HD
        out = attention(
            queries[:, left : left + wide], whole[f], place, doc_ids, block_mask, 2, skip
        )
        left += wide
        attn.append(out)
        up = down = out
        for s in range(3):
            up = line(up, 1)
            down = line(down, -1)
            ups[s].append(up)
            downs[s].append(down)

    low = chip < 2
    zero = jnp.int32(0)
    pair = [out_weight, w_other]

    own = project("full", zero, zero, attn, [], pair)
    goes = [
        ((2 * z + k) * 2 + (1 - z // 2), (2 * z + k) * 2 + z // 2)
        for z in range(4)
        for k in range(2)
    ]
    moved = lax.ppermute(own, LANES, goes)
    arrays = []
    keep, send = project("split", ~low, side, downs[0], ups[0], pair, twin=True)
    both = keep + across(send)
    arrays += send_back("first", both[: tok // 2])
    arrays += send_back("again", both[tok // 2 :])
    keep, send = project("split", ~low, side, downs[1], ups[1], pair)
    arrays += send_back("second", keep + across(send))
    own = own + moved
    out = collect(chip, side, core, arrays + [own], tok, queries.shape[1])
    early = project("part", ~low, side, downs[2][:-1], ups[2][:-1], pair, row=0)
    cols = out_weight.shape[1]
    thirds = []
    for o in range(2):
        keep, send = project(
            "rest",
            ~low,
            side,
            downs[2][-1:],
            ups[2][-1:],
            pair[o : o + 1],
            row=1,
            part=(early, o * cols // 512),
        )
        thirds.append(keep + across(send))
    last = send_back("third", jnp.concatenate(thirds, axis=1))
    return finish(chip, side, core, last, out)


def gathered(queries, keys, values, doc_ids, block_mask, out_weight):
    place = lax.axis_index("ctx")
    n = lax.axis_size("ctx")
    kv = lax.all_gather(parts_of(keys, values, [keys.shape[1] // HD])[0], "ctx", axis=0)
    flip = place + 1 - 2 * (place % 2)

    def of(start):
        return [
            lax.dynamic_index_in_dim(kv, (start - 2 * s + n) % n, 0, keepdims=False)
            for s in range(n // 2)
        ]

    attn = attention(queries, of(place) + of(flip), place, doc_ids, block_mask, 2)
    partial_out = jnp.dot(
        attn,
        lax.all_gather(out_weight, "ctx", axis=1, tiled=True),
        preferred_element_type=jnp.float32,
    )
    return lax.psum_scatter(
        partial_out.astype(jnp.bfloat16), "heads", scatter_dimension=1, tiled=True
    )


def solution(mesh):
    in_specs = (
        P(("groups", "ctx"), "heads"),
        P(("groups", "ctx"), "heads"),
        P(("groups", "ctx"), "heads"),
        P("groups"),
        P("groups", None),
        P("heads", "ctx"),
    )
    out_specs = P(("groups", "ctx"), "heads")
    short = mesh.shape["ctx"] == 8 and mesh.shape["heads"] == 2

    def body(*args):
        return (on_line if short else gathered)(*args)

    return jax.shard_map(
        body, mesh=mesh, in_specs=in_specs, out_specs=out_specs, check_vma=False
    )
```
